32 devices in a mesh: trans: 8 (over y, x, core), pw: 4 (over z).
Axes of the slice: x: 2, y: 2, z: 4, core: 2. Of those that a mesh axis runs over, the one named last changes fastest.
Arguments:
- densities: bfloat16 [4096, 65536], P('trans', 'pw'), may hold values from -6 to 6
- eigen_basis: bfloat16 [65536, 768], P('pw', 'trans'), may hold values from -0.0234375 to 0.0234375
- energies: float32 [4096], P('trans'), may hold values from 0.2 to 4
- frequencies: float32 [8], P('pw'), may hold values from 0.05 to 6
Outputs:
- polarizability: float32 [8, 768, 768], P('pw', 'trans')
The draws below stay inside these ranges and needn't reach their ends.
All inputs are finite; a program needn't handle non-finite values.
Results may differ from the reference program's by a relative error of at most 0.004.
Values may be sent and summed in bfloat16 or wider, within the bound.
No kernel may reach another device: no remote copies, remote signals or barrier semaphores. Data moves between devices by JAX's collectives and lax.ppermute only.
A program may use at most 128 MiB of HBM per device.

```python
import math
import jax
import jax.numpy as jnp
from jax import lax

G = 65536
K = 768
W = 8
TRANSITIONS = 4096


def steps_of(stream_key, extent, split, low, largest):
    def one(axis_at, shards_of):
        heights = jax.random.uniform(jax.random.fold_in(jax.random.fold_in(stream_key, 6), axis_at), (shards_of,), jnp.float32, low / len(split), largest / len(split))
        return jnp.repeat(jnp.exp(heights), extent[axis_at] // shards_of).reshape((-1,) + (1,) * (len(extent) - axis_at - 1))

    gain = one(*split[0])
    for cut in split[1:]:
        gain = gain * one(*cut)
    return gain


def noise(rng, dims, scale, bound, shards=(), kind=jnp.bfloat16):
    array = jax.random.normal(rng, dims, jnp.float32) * scale
    if len(shards) > 0:
        array = steps_of(rng, dims, shards, -0.22, 0.18) * array
    return jnp.clip(array, min=-bound, max=bound).astype(kind)


def setup_inputs(seed: int = 0) -> dict:
    seeds = jax.random.split(jax.random.key(seed), 5)
    return {
        "densities": noise(seeds[0], (TRANSITIONS, G), 1.0, 6.0, ((0, 8), (1, 4))),
        "eigen_basis": noise(seeds[1], (G, K), G ** -0.5, 0.0234375, ((0, 4), (1, 8))),
        "energies": jnp.clip(jnp.exp(math.log(4.0) - 2.9957323 * jax.random.uniform(seeds[2], (TRANSITIONS,), jnp.float32) ** steps_of(seeds[2], (TRANSITIONS,), ((0, 8),), -0.2, 0.2)), 0.2, 4.0),
        "frequencies": jnp.clip(jnp.exp(math.log(6.0) - 4.787492 * jax.random.uniform(seeds[3], (W,), jnp.float32) ** steps_of(seeds[3], (W,), ((0, 4),), -0.2, 0.2)), 0.05, 6.0),
    }


def reference(densities, eigen_basis, energies, frequencies):
    projected = jnp.dot(densities, eigen_basis, preferred_element_type=jnp.float32).astype(jnp.bfloat16)
    prefactor = 1.0 / math.sqrt(energies.shape[0])

    def single(freq):
        factors = -4.0 * energies / (energies * energies + freq * freq) * prefactor
        weighted = (projected.astype(jnp.float32) * factors[:, None]).astype(jnp.bfloat16)
        return lax.dot_general(weighted, projected, (((0,), (0,)), ((), ())), preferred_element_type=jnp.float32)
    return lax.map(single, frequencies)
```

```python
import functools
import math

import jax
import jax.numpy as jnp
from jax import lax
from jax.experimental import pallas as pl
from jax.experimental.pallas import tpu as pltpu
from jax.sharding import PartitionSpec as P


NT = (((1,), (1,)), ((), ()))
VMEM = pl.BlockSpec(memory_space=pltpu.VMEM)
SMEM = pl.BlockSpec(memory_space=pltpu.SMEM)
HBM = pl.BlockSpec(memory_space=pltpu.HBM)
WIRE = jnp.bfloat16
SLOTS = 2


def reverse_bits(value, bits):
    return sum(((value >> i) & 1) << (bits - 1 - i) for i in range(bits))


def frame_hop(count, bits, bit):
    return [(d, d ^ (2 << (bits - 1 - bit if d & 1 else bit))) for d in range(count)]


def row_sections(rows):
    units = rows // 16
    if rows % 16 or units < 3:
        return [(0, rows)]
    last = max(1, units // 6)
    middle = max(1, units // 3)
    sizes = [16 * (units - middle - last), 16 * middle, 16 * last]
    starts = [0, sizes[0], sizes[0] + sizes[1]]
    return list(zip(starts, sizes))


def project_kernel(tile, *refs):
    *pieces, densities, out, held, arrived = refs
    steps = densities.shape[1] // tile

    def fetch(i, slot):
        at = pl.ds(pl.multiple_of(i * tile, tile), tile)
        return pltpu.make_async_copy(densities.at[:, at], held.at[slot], arrived.at[slot])

    for i in range(min(SLOTS - 1, steps)):
        fetch(i, i).start()
    out[...] = jnp.zeros_like(out)

    def step(i, carry):
        slot = lax.rem(i, SLOTS)
        ahead = i + SLOTS - 1

        @pl.when(ahead < steps)
        def _():
            fetch(ahead, lax.rem(ahead, SLOTS)).start()

        fetch(i, slot).wait()
        at = pl.ds(pl.multiple_of(i * tile, tile), tile)
        basis = jnp.concatenate([piece[:, at] for piece in pieces], axis=0)
        out[...] += lax.dot_general(basis, held[slot], NT, preferred_element_type=jnp.float32)
        return carry

    lax.fori_loop(0, steps, step, 0)


def project(pieces, densities):
    rows = len(pieces) * pieces[0].shape[0]
    states, waves = densities.shape
    tile = math.gcd(waves, 2048)
    return pl.pallas_call(
        functools.partial(project_kernel, tile),
        out_shape=jax.ShapeDtypeStruct((rows, states), jnp.float32),
        in_specs=[VMEM] * len(pieces) + [HBM],
        out_specs=VMEM,
        scratch_shapes=[
            pltpu.VMEM((SLOTS, states, tile), densities.dtype),
            pltpu.SemaphoreType.DMA((SLOTS,)),
        ],
        compiler_params=pltpu.CompilerParams(vmem_limit_bytes=34 << 20),
        cost_estimate=pl.CostEstimate(
            flops=2 * rows * states * waves,
            bytes_accessed=2 * waves * (rows + states),
            transcendentals=0,
        ),
    )(*pieces, densities)


def summed(value, axis):
    count = lax.axis_size(axis)
    if count & (count - 1):
        return lax.psum(value, axis)
    for i in range(count.bit_length() - 1):
        pairs = [(d, d ^ (1 << i)) for d in range(count)]
        moved = lax.ppermute(value.astype(WIRE), axis, pairs)
        value = value + moved.astype(jnp.float32)
    return value


def terms_kernel(starts, place, factors, *refs):
    *sections, kept, sent, ordered, weighted = refs
    freqs = factors.shape[0]
    spots, rows = kept.shape[1:3]
    for section, start in zip(sections, starts):
        size = section.shape[1]
        for i in range(2 * spots):
            value = section[i].astype(jnp.float32)
            at = pl.multiple_of(place[i] * rows + start, 8)
            ordered[pl.ds(at, size), :] = value
            for w in range(freqs):
                at = (w * spots + i // 2) * rows + start
                weighted[i % 2, at : at + size, :] = (value * factors[w : w + 1, :]).astype(
                    jnp.bfloat16
                )
    right = ordered[...].astype(jnp.bfloat16)
    for core, out in ((1, sent), (0, kept)):
        term = lax.dot_general(weighted[core], right, NT, preferred_element_type=jnp.float32)
        out[...] = term.reshape(out.shape).astype(out.dtype)


def on_device(densities, eigen_basis, energies, frequencies):
    count = lax.axis_size("trans")
    bits = count.bit_length() - 2
    states = densities.shape[0]
    rows = eigen_basis.shape[1]
    subspace = rows * count
    me = lax.axis_index("trans")
    basis = eigen_basis.T
    spots = 1 << bits
    core_hop = [(d, d ^ 1) for d in range(count)]
    hops = [frame_hop(count, bits, bit) for bit in range(bits)]

    sections, starts = [], []
    for start, size in row_sections(rows):
        mine = [basis[start : start + size]]
        for spot in range(1, spots):
            low = (spot & -spot).bit_length() - 1
            mine.append(lax.ppermute(mine[spot & (spot - 1)], "trans", hops[low]))
        theirs = [lax.ppermute(mine[spot], "trans", core_hop) for spot in range(spots)]
        pieces = []
        for spot in range(spots):
            pieces += [mine[spot], theirs[reverse_bits(spot, bits)]]
        partial = project(pieces, densities)
        projected = summed(partial, "pw").astype(jnp.bfloat16)
        sections.append(projected.reshape(count, size, states))
        starts.append(start)

    prefactor = 1.0 / math.sqrt(states * count)
    factors = (
        -4.0
        * energies[None, :]
        / (energies[None, :] * energies[None, :] + frequencies[:, None] * frequencies[:, None])
        * prefactor
    )
    freqs = frequencies.shape[0]
    place = []
    for i in range(count):
        up, core = i >> 1, i & 1
        even = (up << 1) | core
        odd = (reverse_bits(up, bits) << 1) | core
        place.append(me ^ jnp.where(me & 1, odd, even))
    kept, sent = pl.pallas_call(
        functools.partial(terms_kernel, starts),
        out_shape=(
            jax.ShapeDtypeStruct((freqs, spots, rows, subspace), jnp.float32),
            jax.ShapeDtypeStruct((freqs, spots, rows, subspace), WIRE),
        ),
        in_specs=[SMEM, VMEM] + [VMEM] * len(sections),
        out_specs=(VMEM, VMEM),
        scratch_shapes=[
            pltpu.VMEM((subspace, states), jnp.float32),
            pltpu.VMEM((2, freqs * spots * rows, states), jnp.bfloat16),
        ],
        compiler_params=pltpu.CompilerParams(vmem_limit_bytes=30 << 20),
    )(jnp.stack(place).astype(jnp.int32), factors, *sections)

    got = lax.ppermute(sent, "trans", core_hop)
    order = [reverse_bits(spot, bits) for spot in range(spots)]
    total = [kept[:, i] + got[:, order[i]].astype(jnp.float32) for i in range(spots)]
    for bit in range(bits - 1, -1, -1):
        half = 1 << bit
        away = jnp.stack(total[half:]).astype(WIRE)
        got = lax.ppermute(away, "trans", hops[bit])
        total = [total[i] + got[i].astype(jnp.float32) for i in range(half)]
    return total[0]


def solution(mesh):
    placed = (P("trans", "pw"), P("pw", "trans"), P("trans"), P("pw"))
    return jax.shard_map(
        on_device, mesh=mesh, in_specs=placed, out_specs=P("pw", "trans", None), check_vma=False
    )
```

```python
import functools
import math

import jax
import jax.numpy as jnp
from jax import lax
from jax.experimental import pallas as pl
from jax.experimental.pallas import tpu as pltpu
from jax.sharding import PartitionSpec as P


NT = (((1,), (1,)), ((), ()))
VMEM = pl.BlockSpec(memory_space=pltpu.VMEM)
SMEM = pl.BlockSpec(memory_space=pltpu.SMEM)
HBM = pl.BlockSpec(memory_space=pltpu.HBM)
WIRE = jnp.bfloat16
SLOTS = 3


def reverse_bits(value, bits):
    return sum(((value >> i) & 1) << (bits - 1 - i) for i in range(bits))


def frame_hop(count, bits, bit):
    return [(d, d ^ (2 << (bits - 1 - bit if d & 1 else bit))) for d in range(count)]


def row_sections(rows):
    units = rows // 16
    if rows % 16 or units < 4:
        return [(0, rows)]
    last = max(1, units // 6)
    rest = units - 2 * last
    sizes = [16 * (rest - rest // 2), 16 * (rest // 2), 16 * last, 16 * last]
    return [(sum(sizes[:i]), size) for i, size in enumerate(sizes)]


def project_kernel(tile, *refs):
    *pieces, densities, out, held, arrived = refs
    steps = densities.shape[1] // tile

    def fetch(i, slot):
        at = pl.ds(pl.multiple_of(i * tile, tile), tile)
        return pltpu.make_async_copy(densities.at[:, at], held.at[slot], arrived.at[slot])

    for i in range(min(SLOTS - 1, steps)):
        fetch(i, i).start()
    out[...] = jnp.zeros_like(out)

    def step(i, carry):
        slot = lax.rem(i, SLOTS)
        ahead = i + SLOTS - 1

        @pl.when(ahead < steps)
        def _():
            fetch(ahead, lax.rem(ahead, SLOTS)).start()

        fetch(i, slot).wait()
        at = pl.ds(pl.multiple_of(i * tile, tile), tile)
        basis = jnp.concatenate([piece[:, at] for piece in pieces], axis=0)
        out[...] += lax.dot_general(basis, held[slot], NT, preferred_element_type=jnp.float32)
        return carry

    lax.fori_loop(0, steps, step, 0)


def project(pieces, densities):
    rows = len(pieces) * pieces[0].shape[0]
    states, waves = densities.shape
    tile = math.gcd(waves, 2048)
    return pl.pallas_call(
        functools.partial(project_kernel, tile),
        out_shape=jax.ShapeDtypeStruct((rows, states), jnp.float32),
        in_specs=[VMEM] * len(pieces) + [HBM],
        out_specs=VMEM,
        scratch_shapes=[
            pltpu.VMEM((SLOTS, states, tile), densities.dtype),
            pltpu.SemaphoreType.DMA((SLOTS,)),
        ],
        compiler_params=pltpu.CompilerParams(vmem_limit_bytes=34 << 20),
        cost_estimate=pl.CostEstimate(
            flops=2 * rows * states * waves,
            bytes_accessed=2 * waves * (rows + states),
            transcendentals=0,
        ),
    )(*pieces, densities)


def summed(value, axis):
    count = lax.axis_size(axis)
    if count & (count - 1):
        return lax.psum(value, axis)
    for i in range(count.bit_length() - 1):
        pairs = [(d, d ^ (1 << i)) for d in range(count)]
        moved = lax.ppermute(value.astype(WIRE), axis, pairs)
        value = value + moved.astype(jnp.float32)
    return value


def terms_kernel(starts, place, factors, *refs):
    *sections, kept, sent, ordered, weighted = refs
    freqs = factors.shape[0]
    spots, rows = kept.shape[1:3]
    for section, start in zip(sections, starts):
        size = section.shape[1]
        for i in range(2 * spots):
            value = section[i].astype(jnp.float32)
            at = pl.multiple_of(place[i] * rows + start, 8)
            ordered[pl.ds(at, size), :] = value
            for w in range(freqs):
                at = (w * spots + i // 2) * rows + start
                weighted[i % 2, at : at + size, :] = (value * factors[w : w + 1, :]).astype(
                    jnp.bfloat16
                )
    right = ordered[...].astype(jnp.bfloat16)
    for core, out in ((1, sent), (0, kept)):
        term = lax.dot_general(weighted[core], right, NT, preferred_element_type=jnp.float32)
        out[...] = term.reshape(out.shape).astype(out.dtype)


def on_device(densities, eigen_basis, energies, frequencies):
    count = lax.axis_size("trans")
    bits = count.bit_length() - 2
    states = densities.shape[0]
    rows = eigen_basis.shape[1]
    subspace = rows * count
    me = lax.axis_index("trans")
    basis = eigen_basis.T
    spots = 1 << bits
    core_hop = [(d, d ^ 1) for d in range(count)]
    hops = [frame_hop(count, bits, bit) for bit in range(bits)]

    sections, starts = [], []
    for start, size in row_sections(rows):
        mine = [basis[start : start + size]]
        for spot in range(1, spots):
            low = (spot & -spot).bit_length() - 1
            mine.append(lax.ppermute(mine[spot & (spot - 1)], "trans", hops[low]))
        theirs = [lax.ppermute(mine[spot], "trans", core_hop) for spot in range(spots)]
        pieces = []
        for spot in range(spots):
            pieces += [mine[spot], theirs[reverse_bits(spot, bits)]]
        partial = project(pieces, densities)
        projected = summed(partial, "pw").astype(jnp.bfloat16)
        sections.append(projected.reshape(count, size, states))
        starts.append(start)

    prefactor = 1.0 / math.sqrt(states * count)
    factors = (
        -4.0
        * energies[None, :]
        / (energies[None, :] * energies[None, :] + frequencies[:, None] * frequencies[:, None])
        * prefactor
    )
    freqs = frequencies.shape[0]
    place = []
    for i in range(count):
        up, core = i >> 1, i & 1
        even = (up << 1) | core
        odd = (reverse_bits(up, bits) << 1) | core
        place.append(me ^ jnp.where(me & 1, odd, even))
    kept, sent = pl.pallas_call(
        functools.partial(terms_kernel, starts),
        out_shape=(
            jax.ShapeDtypeStruct((freqs, spots, rows, subspace), jnp.float32),
            jax.ShapeDtypeStruct((freqs, spots, rows, subspace), WIRE),
        ),
        in_specs=[SMEM, VMEM] + [VMEM] * len(sections),
        out_specs=(VMEM, VMEM),
        scratch_shapes=[
            pltpu.VMEM((subspace, states), jnp.float32),
            pltpu.VMEM((2, freqs * spots * rows, states), jnp.bfloat16),
        ],
        compiler_params=pltpu.CompilerParams(vmem_limit_bytes=30 << 20),
    )(jnp.stack(place).astype(jnp.int32), factors, *sections)

    got = lax.ppermute(sent, "trans", core_hop)
    order = [reverse_bits(spot, bits) for spot in range(spots)]
    total = [kept[:, i] + got[:, order[i]].astype(jnp.float32) for i in range(spots)]
    for bit in range(bits - 1, -1, -1):
        half = 1 << bit
        away = jnp.stack(total[half:]).astype(WIRE)
        got = lax.ppermute(away, "trans", hops[bit])
        total = [total[i] + got[i].astype(jnp.float32) for i in range(half)]
    return total[0]


def solution(mesh):
    placed = (P("trans", "pw"), P("pw", "trans"), P("trans"), P("pw"))
    return jax.shard_map(
        on_device, mesh=mesh, in_specs=placed, out_specs=P("pw", "trans", None), check_vma=False
    )
```

```python
import functools
import math

import jax
import jax.numpy as jnp
from jax import lax
from jax.experimental import pallas as pl
from jax.experimental.pallas import tpu as pltpu
from jax.sharding import PartitionSpec as P


NT = (((1,), (1,)), ((), ()))
VMEM = pl.BlockSpec(memory_space=pltpu.VMEM)
SMEM = pl.BlockSpec(memory_space=pltpu.SMEM)
HBM = pl.BlockSpec(memory_space=pltpu.HBM)
WIRE = jnp.bfloat16
SLOTS = 3


def reverse_bits(value, bits):
    return sum(((value >> i) & 1) << (bits - 1 - i) for i in range(bits))


def frame_hop(count, bits, bit):
    return [(d, d ^ (2 << (bits - 1 - bit if d & 1 else bit))) for d in range(count)]


def row_sections(rows):
    units = rows // 16
    if rows % 16 or units < 6:
        return [(0, rows)], [[0]]
    last = units // 6
    sizes = [16 * (units - 4 * last)] + [16 * last] * 4
    return [(sum(sizes[:i]), size) for i, size in enumerate(sizes)], [[0, 1, 2], [3], [4]]


def project_kernel(tile, *refs):
    *pieces, densities, out, held, arrived = refs
    steps = densities.shape[1] // tile

    def fetch(i, slot):
        at = pl.ds(pl.multiple_of(i * tile, tile), tile)
        return pltpu.make_async_copy(densities.at[:, at], held.at[slot], arrived.at[slot])

    for i in range(min(SLOTS - 1, steps)):
        fetch(i, i).start()
    out[...] = jnp.zeros_like(out)

    def step(i, carry):
        slot = lax.rem(i, SLOTS)
        ahead = i + SLOTS - 1

        @pl.when(ahead < steps)
        def _():
            fetch(ahead, lax.rem(ahead, SLOTS)).start()

        fetch(i, slot).wait()
        at = pl.ds(pl.multiple_of(i * tile, tile), tile)
        basis = jnp.concatenate([piece[:, at] for piece in pieces], axis=0)
        out[...] += lax.dot_general(basis, held[slot], NT, preferred_element_type=jnp.float32)
        return carry

    lax.fori_loop(0, steps, step, 0)


def project(pieces, densities):
    rows = len(pieces) * pieces[0].shape[0]
    states, waves = densities.shape
    tile = math.gcd(waves, 2048)
    return pl.pallas_call(
        functools.partial(project_kernel, tile),
        out_shape=jax.ShapeDtypeStruct((rows, states), jnp.float32),
        in_specs=[VMEM] * len(pieces) + [HBM],
        out_specs=VMEM,
        scratch_shapes=[
            pltpu.VMEM((SLOTS, states, tile), densities.dtype),
            pltpu.SemaphoreType.DMA((SLOTS,)),
        ],
        compiler_params=pltpu.CompilerParams(vmem_limit_bytes=34 << 20),
        cost_estimate=pl.CostEstimate(
            flops=2 * rows * states * waves,
            bytes_accessed=2 * waves * (rows + states),
            transcendentals=0,
        ),
    )(*pieces, densities)


def summed(value, axis):
    count = lax.axis_size(axis)
    if count & (count - 1):
        return lax.psum(value, axis)
    for i in range(count.bit_length() - 1):
        pairs = [(d, d ^ (1 << i)) for d in range(count)]
        moved = lax.ppermute(value.astype(WIRE), axis, pairs)
        value = value + moved.astype(jnp.float32)
    return value


def terms_kernel(bits, starts, prefactor, device, frequencies, *refs):
    sources = 4
    energies, refs = refs[:sources], refs[sources:]
    *groups, kept, sent, ordered, weighted = refs
    freqs = frequencies.shape[0]
    count = groups[0].shape[0]
    half = 1 << (bits - 1)
    rows = kept.shape[-2]
    me = device[0]
    across = me ^ jnp.where(me & 1, 2, 2 * half)
    owner = [me, me ^ 1, across, across ^ 1]
    held = [
        lambda spot: 2 * spot,
        lambda spot: 2 * reverse_bits(spot, bits) + 1,
        lambda spot: 2 * (spot ^ half),
        lambda spot: 2 * reverse_bits(spot ^ half, bits) + 1,
    ]
    total = [None, None]
    for q in range(sources):
        energy = energies[q][...]
        factors = []
        for w in range(freqs):
            square = frequencies[w] * frequencies[w]
            factors.append(-4.0 * energy / (energy * energy + square) * prefactor)
        for group, start in zip(groups[q::sources], starts):
            size = group.shape[1]
            for i in range(count):
                up, core = i >> 1, i & 1
                even, odd = 2 * up + core, 2 * reverse_bits(up, bits) + core
                piece = owner[q] ^ jnp.where(owner[q] & 1, odd, even)
                at = pl.multiple_of(piece * rows + start, 8)
                ordered[q % 2, pl.ds(at, size), :] = group[i].astype(jnp.float32)
            for spot in range(half):
                value = group[held[q](spot)].astype(jnp.float32)
                for w in range(freqs):
                    at = (spot * freqs + w) * rows + start
                    weighted[q % 2, at : at + size, :] = (value * factors[w]).astype(jnp.bfloat16)
        right = ordered[q % 2].astype(jnp.bfloat16)
        own = freqs * rows
        for k, part in enumerate((slice(own, half * own), slice(0, own))):
            if part.stop > part.start:
                term = lax.dot_general(
                    weighted[q % 2, part, :], right, NT, preferred_element_type=jnp.float32
                )
                total[k] = term if q == 0 else total[k] + term
    if half > 1:
        sent[...] = total[0].reshape(sent.shape)
    kept[...] = total[1].reshape(kept.shape)


def on_device(densities, eigen_basis, energies, frequencies):
    count = lax.axis_size("trans")
    bits = count.bit_length() - 2
    half = 1 << (bits - 1)
    states = densities.shape[0]
    rows = eigen_basis.shape[1]
    subspace = rows * count
    basis = eigen_basis.T
    spots = 1 << bits
    core_hop = [(d, d ^ 1) for d in range(count)]
    hops = [frame_hop(count, bits, bit) for bit in range(bits)]

    def from_sources(value):
        beside = lax.ppermute(value, "trans", core_hop)
        across = lax.ppermute(value, "trans", hops[-1])
        return [value, beside, across, lax.ppermute(beside, "trans", hops[-1])]

    sections, groups = row_sections(rows)
    energy = [value.reshape(1, states) for value in from_sources(energies)]
    prefactor = 1.0 / math.sqrt(states * count)

    projected = []
    for start, size in sections:
        mine = [basis[start : start + size]]
        for spot in range(1, spots):
            low = (spot & -spot).bit_length() - 1
            mine.append(lax.ppermute(mine[spot & (spot - 1)], "trans", hops[low]))
        theirs = [lax.ppermute(mine[spot], "trans", core_hop) for spot in range(spots)]
        pieces = []
        for spot in range(spots):
            pieces += [mine[spot], theirs[reverse_bits(spot, bits)]]
        partial = project(pieces, densities)
        projected.append(summed(partial, "pw").astype(jnp.bfloat16))

    operands, starts = [], []
    for group in groups:
        value = [projected[i].reshape(count, sections[i][1], states) for i in group]
        operands += from_sources(jnp.concatenate(value, axis=1))
        starts.append(sections[group[0]][0])
    freqs = frequencies.shape[0]
    kept, sent = pl.pallas_call(
        functools.partial(terms_kernel, bits, starts, prefactor),
        out_shape=(
            jax.ShapeDtypeStruct((freqs, rows, subspace), jnp.float32),
            jax.ShapeDtypeStruct((max(half - 1, 1), freqs, rows, subspace), jnp.float32),
        ),
        in_specs=[SMEM] * 2 + [VMEM] * (len(energy) + len(operands)),
        out_specs=(VMEM, VMEM),
        scratch_shapes=[
            pltpu.VMEM((2, subspace, states), jnp.float32),
            pltpu.VMEM((2, half * freqs * rows, states), jnp.bfloat16),
        ],
        compiler_params=pltpu.CompilerParams(vmem_limit_bytes=30 << 20),
    )(lax.axis_index("trans").astype(jnp.int32).reshape(1), frequencies, *energy, *operands)

    total = [kept] + [sent[i] for i in range(half - 1)]
    for bit in range(bits - 2, -1, -1):
        near = 1 << bit
        away = jnp.stack(total[near:]).astype(WIRE)
        got = lax.ppermute(away, "trans", hops[bit])
        total = [total[i] + got[i].astype(jnp.float32) for i in range(near)]
    return total[0]


def solution(mesh):
    placed = (P("trans", "pw"), P("pw", "trans"), P("trans"), P("pw"))
    return jax.shard_map(
        on_device, mesh=mesh, in_specs=placed, out_specs=P("pw", "trans", None), check_vma=False
    )
```

```python
import functools
import math

import jax
import jax.numpy as jnp
from jax import lax
from jax.experimental import pallas as pl
from jax.experimental.pallas import tpu as pltpu
from jax.sharding import PartitionSpec as P


NT = (((1,), (1,)), ((), ()))
VMEM = pl.BlockSpec(memory_space=pltpu.VMEM)
SMEM = pl.BlockSpec(memory_space=pltpu.SMEM)
HBM = pl.BlockSpec(memory_space=pltpu.HBM)
WIRE = jnp.bfloat16
SLOTS = 3


def reverse_bits(value, bits):
    return sum(((value >> i) & 1) << (bits - 1 - i) for i in range(bits))


def frame_hop(count, bits, bit):
    return [(d, d ^ (2 << (bits - 1 - bit if d & 1 else bit))) for d in range(count)]


def row_sections(rows):
    units = rows // 16
    if rows % 16 or units < 3:
        return [(0, rows, 1, 1)]
    last = 16 * (units // 3)
    blocks = 1 if last % 32 else 2
    return [(0, rows - 2 * last, 1, 1), (rows - 2 * last, last, 1, 1), (rows - last, last, 2, blocks)]


def project_kernel(tile, first, blocks, resumed, *refs):
    *pieces, densities = refs[: -blocks - 3]
    outs, (held, arrived, total) = refs[-blocks - 3 : -3], refs[-3:]
    pieces, before = pieces[: len(pieces) - resumed], pieces[len(pieces) - resumed :]
    steps = pieces[0].shape[1] // tile
    size = pieces[0].shape[0] // blocks
    rows = size * len(pieces)

    def fetch(i, slot):
        at = pl.ds(pl.multiple_of(first + i * tile, tile), tile)
        return pltpu.make_async_copy(densities.at[:, at], held.at[slot], arrived.at[slot])

    for i in range(min(SLOTS - 1, steps)):
        fetch(i, i).start()
    for block in range(blocks):
        at = slice(block * rows, block * rows + rows)
        total[at, :] = before[block][...] if resumed else jnp.zeros((rows, total.shape[1]), total.dtype)

    def step(i, carry):
        slot = lax.rem(i, SLOTS)
        ahead = i + SLOTS - 1

        @pl.when(ahead < steps)
        def _():
            fetch(ahead, lax.rem(ahead, SLOTS)).start()

        fetch(i, slot).wait()
        at = pl.ds(pl.multiple_of(i * tile, tile), tile)
        basis = jnp.concatenate(
            [piece[b * size : b * size + size, at] for b in range(blocks) for piece in pieces], axis=0
        )
        total[...] += lax.dot_general(basis, held[slot], NT, preferred_element_type=jnp.float32)
        return carry

    lax.fori_loop(0, steps, step, 0)
    for block in range(blocks):
        outs[block][...] = total[block * rows : block * rows + rows, :]


def project(pieces, densities, first, blocks, before):
    rows = len(pieces) * pieces[0].shape[0]
    states, waves = densities.shape[0], pieces[0].shape[1]
    tile = math.gcd(waves, 2048)
    return pl.pallas_call(
        functools.partial(project_kernel, tile, first, blocks, len(before)),
        out_shape=[jax.ShapeDtypeStruct((rows // blocks, states), jnp.float32)] * blocks,
        in_specs=[VMEM] * (len(pieces) + len(before)) + [HBM],
        out_specs=[VMEM] * blocks,
        scratch_shapes=[
            pltpu.VMEM((SLOTS, states, tile), densities.dtype),
            pltpu.SemaphoreType.DMA((SLOTS,)),
            pltpu.VMEM((rows, states), jnp.float32),
        ],
        compiler_params=pltpu.CompilerParams(vmem_limit_bytes=34 << 20),
        cost_estimate=pl.CostEstimate(
            flops=2 * rows * states * waves,
            bytes_accessed=2 * waves * (rows + states),
            transcendentals=0,
        ),
    )(*pieces, *before, densities)


def summed(value, axis):
    count = lax.axis_size(axis)
    if count & (count - 1):
        return lax.psum(value, axis)
    for i in range(count.bit_length() - 1):
        pairs = [(d, d ^ (1 << i)) for d in range(count)]
        moved = lax.ppermute(value.astype(WIRE), axis, pairs)
        value = value + moved.astype(jnp.float32)
    return value


def terms_kernel(bits, starts, prefactor, device, frequencies, *refs):
    sources = 4
    energies, refs = refs[:sources], refs[sources:]
    *groups, kept, sent, ordered, weighted = refs
    freqs = frequencies.shape[0]
    count = groups[0].shape[0]
    half = 1 << (bits - 1)
    rows = kept.shape[-2]
    me = device[0]
    across = me ^ jnp.where(me & 1, 2, 2 * half)
    owner = [me, me ^ 1, across, across ^ 1]
    held = [
        lambda spot: 2 * spot,
        lambda spot: 2 * reverse_bits(spot, bits) + 1,
        lambda spot: 2 * (spot ^ half),
        lambda spot: 2 * reverse_bits(spot ^ half, bits) + 1,
    ]
    total = [None, None]
    for q in range(sources):
        energy = energies[q][...]
        factors = []
        for w in range(freqs):
            square = frequencies[w] * frequencies[w]
            factors.append(-4.0 * energy / (energy * energy + square) * prefactor)
        for group, start in zip(groups[q::sources], starts):
            size = group.shape[1]
            for i in range(count):
                up, core = i >> 1, i & 1
                even, odd = 2 * up + core, 2 * reverse_bits(up, bits) + core
                piece = owner[q] ^ jnp.where(owner[q] & 1, odd, even)
                at = pl.multiple_of(piece * rows + start, 8)
                ordered[q % 2, pl.ds(at, size), :] = group[i].astype(jnp.float32)
            for spot in range(half):
                value = group[held[q](spot)].astype(jnp.float32)
                for w in range(freqs):
                    at = (spot * freqs + w) * rows + start
                    weighted[q % 2, at : at + size, :] = (value * factors[w]).astype(jnp.bfloat16)
        right = ordered[q % 2].astype(jnp.bfloat16)
        own = freqs * rows
        for k, part in enumerate((slice(own, half * own), slice(0, own))):
            if part.stop > part.start:
                term = lax.dot_general(
                    weighted[q % 2, part, :], right, NT, preferred_element_type=jnp.float32
                )
                total[k] = term if q == 0 else total[k] + term
    if half > 1:
        sent[...] = total[0].reshape(sent.shape)
    kept[...] = total[1].reshape(kept.shape)


def on_device(densities, eigen_basis, energies, frequencies):
    count = lax.axis_size("trans")
    bits = count.bit_length() - 2
    half = 1 << (bits - 1)
    states = densities.shape[0]
    rows = eigen_basis.shape[1]
    subspace = rows * count
    basis = eigen_basis.T
    spots = 1 << bits
    core_hop = [(d, d ^ 1) for d in range(count)]
    hops = [frame_hop(count, bits, bit) for bit in range(bits)]

    direct = [(across ^ 1, d) for d, across in hops[-1]]

    def from_sources(value):
        return [
            value,
            lax.ppermute(value, "trans", core_hop),
            lax.ppermute(value, "trans", hops[-1]),
            lax.ppermute(value, "trans", direct),
        ]

    energy = [value.reshape(1, states) for value in from_sources(energies)]
    prefactor = 1.0 / math.sqrt(states * count)

    operands, starts = [], []
    for start, size, parts, blocks in row_sections(rows):
        waves = basis.shape[1] // parts
        sums = []
        for part in range(parts):
            mine = [basis[start : start + size, part * waves : part * waves + waves]]
            for spot in range(1, spots):
                low = (spot & -spot).bit_length() - 1
                mine.append(lax.ppermute(mine[spot & (spot - 1)], "trans", hops[low]))
            theirs = [lax.ppermute(mine[spot], "trans", core_hop) for spot in range(spots)]
            pieces = []
            for spot in range(spots):
                pieces += [mine[spot], theirs[reverse_bits(spot, bits)]]
            sums = project(pieces, densities, part * waves, blocks, sums)
        for block, value in enumerate(sums):
            projected = summed(value, "pw").astype(jnp.bfloat16)
            operands += from_sources(projected.reshape(count, size // blocks, states))
            starts.append(start + block * (size // blocks))
    freqs = frequencies.shape[0]
    kept, sent = pl.pallas_call(
        functools.partial(terms_kernel, bits, starts, prefactor),
        out_shape=(
            jax.ShapeDtypeStruct((freqs, rows, subspace), jnp.float32),
            jax.ShapeDtypeStruct((max(half - 1, 1), freqs, rows, subspace), jnp.float32),
        ),
        in_specs=[SMEM] * 2 + [VMEM] * (len(energy) + len(operands)),
        out_specs=(VMEM, VMEM),
        scratch_shapes=[
            pltpu.VMEM((2, subspace, states), jnp.float32),
            pltpu.VMEM((2, half * freqs * rows, states), jnp.bfloat16),
        ],
        compiler_params=pltpu.CompilerParams(vmem_limit_bytes=30 << 20),
    )(lax.axis_index("trans").astype(jnp.int32).reshape(1), frequencies, *energy, *operands)

    total = [kept] + [sent[i] for i in range(half - 1)]
    for bit in range(bits - 2, -1, -1):
        near = 1 << bit
        away = jnp.stack(total[near:]).astype(WIRE)
        got = lax.ppermute(away, "trans", hops[bit])
        total = [total[i] + got[i].astype(jnp.float32) for i in range(near)]
    return total[0]


def solution(mesh):
    placed = (P("trans", "pw"), P("pw", "trans"), P("trans"), P("pw"))
    return jax.shard_map(on_device, mesh=mesh, in_specs=placed, out_specs=P("pw", "trans", None), check_vma=False)
```

```python
import functools
import math

import jax
import jax.numpy as jnp
from jax import lax
from jax.experimental import pallas as pl
from jax.experimental.pallas import tpu as pltpu
from jax.sharding import PartitionSpec as P


NT = (((1,), (1,)), ((), ()))
VMEM = pl.BlockSpec(memory_space=pltpu.VMEM)
SMEM = pl.BlockSpec(memory_space=pltpu.SMEM)
HBM = pl.BlockSpec(memory_space=pltpu.HBM)
WIRE = jnp.bfloat16
SLOTS = 3


def reverse_bits(value, bits):
    return sum(((value >> i) & 1) << (bits - 1 - i) for i in range(bits))


def frame_hop(count, bits, bit):
    return [(d, d ^ (2 << (bits - 1 - bit if d & 1 else bit))) for d in range(count)]


def row_sections(rows):
    units = rows // 16
    if rows % 16 or units < 3:
        return [(0, rows, 1, 1)]
    sizes = [16 * (units // 3), 16 * max(1, units // 6)]
    first = rows - sum(sizes)
    return [(0, first, 1, 1), (first, sizes[0], 2, 1), (first + sizes[0], sizes[1], 1, 1)]


def project_kernel(tile, first, blocks, resumed, *refs):
    *pieces, densities = refs[: -blocks - 3]
    outs, (held, arrived, total) = refs[-blocks - 3 : -3], refs[-3:]
    pieces, before = pieces[: len(pieces) - resumed], pieces[len(pieces) - resumed :]
    steps = pieces[0].shape[1] // tile
    size = pieces[0].shape[0] // blocks
    rows = size * len(pieces)

    def fetch(i, slot):
        at = pl.ds(pl.multiple_of(first + i * tile, tile), tile)
        return pltpu.make_async_copy(densities.at[:, at], held.at[slot], arrived.at[slot])

    for i in range(min(SLOTS - 1, steps)):
        fetch(i, i).start()
    for block in range(blocks):
        at = slice(block * rows, block * rows + rows)
        total[at, :] = before[block][...] if resumed else jnp.zeros((rows, total.shape[1]), total.dtype)

    def step(i, carry):
        slot = lax.rem(i, SLOTS)
        ahead = i + SLOTS - 1

        @pl.when(ahead < steps)
        def _():
            fetch(ahead, lax.rem(ahead, SLOTS)).start()

        fetch(i, slot).wait()
        at = pl.ds(pl.multiple_of(i * tile, tile), tile)
        basis = jnp.concatenate(
            [piece[b * size : b * size + size, at] for b in range(blocks) for piece in pieces], axis=0
        )
        total[...] += lax.dot_general(basis, held[slot], NT, preferred_element_type=jnp.float32)
        return carry

    lax.fori_loop(0, steps, step, 0)
    for block in range(blocks):
        outs[block][...] = total[block * rows : block * rows + rows, :]


def project(pieces, densities, first, blocks, before):
    rows = len(pieces) * pieces[0].shape[0]
    states, waves = densities.shape[0], pieces[0].shape[1]
    tile = math.gcd(waves, 2048)
    return pl.pallas_call(
        functools.partial(project_kernel, tile, first, blocks, len(before)),
        out_shape=[jax.ShapeDtypeStruct((rows // blocks, states), jnp.float32)] * blocks,
        in_specs=[VMEM] * (len(pieces) + len(before)) + [HBM],
        out_specs=[VMEM] * blocks,
        scratch_shapes=[
            pltpu.VMEM((SLOTS, states, tile), densities.dtype),
            pltpu.SemaphoreType.DMA((SLOTS,)),
            pltpu.VMEM((rows, states), jnp.float32),
        ],
        compiler_params=pltpu.CompilerParams(vmem_limit_bytes=(46 << 20) - min(rows * waves, 12 << 20)),
        cost_estimate=pl.CostEstimate(
            flops=2 * rows * states * waves,
            bytes_accessed=2 * waves * (rows + states),
            transcendentals=0,
        ),
    )(*pieces, *before, densities)


def summed(value, axis):
    count = lax.axis_size(axis)
    if count & (count - 1):
        return lax.psum(value, axis)
    bits = count.bit_length() - 1
    for bit in reversed(range(bits)):
        pairs = [(d, d ^ (1 << bit)) for d in range(count)]
        moved = lax.ppermute(value.astype(WIRE), axis, pairs)
        value = value + moved.astype(jnp.float32)
    return value


def terms_kernel(bits, starts, prefactor, device, frequencies, *refs):
    sources = 4
    energies, refs = refs[:sources], refs[sources:]
    *groups, kept, sent, ordered, weighted = refs
    freqs = frequencies.shape[0]
    count = groups[0].shape[0]
    half = 1 << (bits - 1)
    rows = kept.shape[-2]
    me = device[0]
    across = me ^ jnp.where(me & 1, 2, 2 * half)
    owner = [me, me ^ 1, across, across ^ 1]
    held = [
        lambda spot: 2 * spot,
        lambda spot: 2 * reverse_bits(spot, bits) + 1,
        lambda spot: 2 * (spot ^ half),
        lambda spot: 2 * reverse_bits(spot ^ half, bits) + 1,
    ]
    total = [None, None]
    for q in range(sources):
        energy = energies[q][...]
        factors = []
        for w in range(freqs):
            square = frequencies[w] * frequencies[w]
            factors.append(-4.0 * energy / (energy * energy + square) * prefactor)
        for group, start in zip(groups[q::sources], starts):
            size = group.shape[1]
            for i in range(count):
                up, core = i >> 1, i & 1
                even, odd = 2 * up + core, 2 * reverse_bits(up, bits) + core
                piece = owner[q] ^ jnp.where(owner[q] & 1, odd, even)
                at = pl.multiple_of(piece * rows + start, 8)
                ordered[q % 2, pl.ds(at, size), :] = group[i].astype(jnp.float32)
            for spot in range(half):
                value = group[held[q](spot)].astype(jnp.float32)
                for w in range(freqs):
                    at = (spot * freqs + w) * rows + start
                    weighted[q % 2, at : at + size, :] = (value * factors[w]).astype(jnp.bfloat16)
        right = ordered[q % 2].astype(jnp.bfloat16)
        own = freqs * rows
        for k, part in enumerate((slice(own, half * own), slice(0, own))):
            if part.stop > part.start:
                term = lax.dot_general(
                    weighted[q % 2, part, :], right, NT, preferred_element_type=jnp.float32
                )
                total[k] = term if q == 0 else total[k] + term
    if half > 1:
        sent[...] = total[0].reshape(sent.shape)
    kept[...] = total[1].reshape(kept.shape)


def on_device(densities, eigen_basis, energies, frequencies):
    count = lax.axis_size("trans")
    bits = count.bit_length() - 2
    half = 1 << (bits - 1)
    states = densities.shape[0]
    rows = eigen_basis.shape[1]
    subspace = rows * count
    basis = eigen_basis.T
    spots = 1 << bits
    core_hop = [(d, d ^ 1) for d in range(count)]
    hops = [frame_hop(count, bits, bit) for bit in range(bits)]

    direct = [(across ^ 1, d) for d, across in hops[-1]]

    def from_sources(value):
        return [
            value,
            lax.ppermute(value, "trans", core_hop),
            lax.ppermute(value, "trans", hops[-1]),
            lax.ppermute(value, "trans", direct),
        ]

    energy = [value.reshape(1, states) for value in from_sources(energies)]
    prefactor = 1.0 / math.sqrt(states * count)

    operands, starts = [], []
    for start, size, parts, blocks in row_sections(rows):
        waves = basis.shape[1] // parts
        sums = []
        for part in range(parts):
            mine = [basis[start : start + size, part * waves : part * waves + waves]]
            for spot in range(1, spots):
                low = (spot & -spot).bit_length() - 1
                mine.append(lax.ppermute(mine[spot & (spot - 1)], "trans", hops[low]))
            theirs = [lax.ppermute(mine[spot], "trans", core_hop) for spot in range(spots)]
            pieces = []
            for spot in range(spots):
                pieces += [mine[spot], theirs[reverse_bits(spot, bits)]]
            sums = project(pieces, densities, part * waves, blocks, sums)
        for block, value in enumerate(sums):
            projected = summed(value, "pw").astype(jnp.bfloat16)
            operands += from_sources(projected.reshape(count, size // blocks, states))
            starts.append(start + block * (size // blocks))
    freqs = frequencies.shape[0]
    kept, sent = pl.pallas_call(
        functools.partial(terms_kernel, bits, starts, prefactor),
        out_shape=(
            jax.ShapeDtypeStruct((freqs, rows, subspace), jnp.float32),
            jax.ShapeDtypeStruct((max(half - 1, 1), freqs, rows, subspace), jnp.float32),
        ),
        in_specs=[SMEM] * 2 + [VMEM] * (len(energy) + len(operands)),
        out_specs=(VMEM, VMEM),
        scratch_shapes=[
            pltpu.VMEM((2, subspace, states), jnp.float32),
            pltpu.VMEM((2, half * freqs * rows, states), jnp.bfloat16),
        ],
        compiler_params=pltpu.CompilerParams(vmem_limit_bytes=30 << 20),
    )(lax.axis_index("trans").astype(jnp.int32).reshape(1), frequencies, *energy, *operands)

    total = [kept] + [sent[i] for i in range(half - 1)]
    for bit in range(bits - 2, -1, -1):
        near = 1 << bit
        away = jnp.stack(total[near:]).astype(WIRE)
        got = lax.ppermute(away, "trans", hops[bit])
        total = [total[i] + got[i].astype(jnp.float32) for i in range(near)]
    return total[0]


def solution(mesh):
    placed = (P("trans", "pw"), P("pw", "trans"), P("trans"), P("pw"))
    return jax.shard_map(on_device, mesh=mesh, in_specs=placed, out_specs=P("pw", "trans", None), check_vma=False)
```

```python
import functools
import math

import jax
import jax.numpy as jnp
from jax import lax
from jax.experimental import pallas as pl
from jax.experimental.pallas import tpu as pltpu
from jax.sharding import PartitionSpec as P


NT = (((1,), (1,)), ((), ()))
VMEM = pl.BlockSpec(memory_space=pltpu.VMEM)
SMEM = pl.BlockSpec(memory_space=pltpu.SMEM)
HBM = pl.BlockSpec(memory_space=pltpu.HBM)
WIRE = jnp.bfloat16
SLOTS = 3


def reverse_bits(value, bits):
    return sum(((value >> i) & 1) << (bits - 1 - i) for i in range(bits))


def frame_hop(count, bits, bit):
    return [(d, d ^ (2 << (bits - 1 - bit if d & 1 else bit))) for d in range(count)]


def row_sections(rows):
    units = rows // 16
    if rows % 16 or units < 3:
        return [(0, rows, 1, 1)]
    sizes = [16 * (units // 3), 16 * max(1, units // 6)]
    first = rows - sum(sizes)
    return [(0, first, 1, 1), (first, sizes[0], 2, 1 if sizes[0] % 32 else 2), (first + sizes[0], sizes[1], 1, 1)]


def project_kernel(tile, first, blocks, resumed, *refs):
    *pieces, densities = refs[: -blocks - 3]
    outs, (held, arrived, total) = refs[-blocks - 3 : -3], refs[-3:]
    pieces, before = pieces[: len(pieces) - resumed], pieces[len(pieces) - resumed :]
    steps = pieces[0].shape[1] // tile
    size = pieces[0].shape[0] // blocks
    rows = size * len(pieces)

    def fetch(i, slot):
        at = pl.ds(pl.multiple_of(first + i * tile, tile), tile)
        return pltpu.make_async_copy(densities.at[:, at], held.at[slot], arrived.at[slot])

    for i in range(min(SLOTS - 1, steps)):
        fetch(i, i).start()
    for block in range(blocks):
        at = slice(block * rows, block * rows + rows)
        total[at, :] = before[block][...] if resumed else jnp.zeros((rows, total.shape[1]), total.dtype)

    def step(i, carry):
        slot = lax.rem(i, SLOTS)
        ahead = i + SLOTS - 1

        @pl.when(ahead < steps)
        def _():
            fetch(ahead, lax.rem(ahead, SLOTS)).start()

        fetch(i, slot).wait()
        at = pl.ds(pl.multiple_of(i * tile, tile), tile)
        basis = jnp.concatenate(
            [piece[b * size : b * size + size, at] for b in range(blocks) for piece in pieces], axis=0
        )
        total[...] += lax.dot_general(basis, held[slot], NT, preferred_element_type=jnp.float32)
        return carry

    lax.fori_loop(0, steps, step, 0)
    for block in range(blocks):
        outs[block][...] = total[block * rows : block * rows + rows, :]


def project(pieces, densities, first, blocks, before):
    rows = len(pieces) * pieces[0].shape[0]
    states, waves = densities.shape[0], pieces[0].shape[1]
    tile = math.gcd(waves, 2048)
    return pl.pallas_call(
        functools.partial(project_kernel, tile, first, blocks, len(before)),
        out_shape=[jax.ShapeDtypeStruct((rows // blocks, states), jnp.float32)] * blocks,
        in_specs=[VMEM] * (len(pieces) + len(before)) + [HBM],
        out_specs=[VMEM] * blocks,
        scratch_shapes=[
            pltpu.VMEM((SLOTS, states, tile), densities.dtype),
            pltpu.SemaphoreType.DMA((SLOTS,)),
            pltpu.VMEM((rows, states), jnp.float32),
        ],
        compiler_params=pltpu.CompilerParams(vmem_limit_bytes=(46 << 20) - min(rows * waves, 12 << 20)),
        cost_estimate=pl.CostEstimate(
            flops=2 * rows * states * waves,
            bytes_accessed=2 * waves * (rows + states),
            transcendentals=0,
        ),
    )(*pieces, *before, densities)


def summed(value, axis, far_first):
    count = lax.axis_size(axis)
    if count & (count - 1):
        return lax.psum(value, axis)
    bits = list(range(count.bit_length() - 1))
    for bit in bits[::-1] if far_first else bits:
        pairs = [(d, d ^ (1 << bit)) for d in range(count)]
        moved = lax.ppermute(value.astype(WIRE), axis, pairs)
        value = value + moved.astype(jnp.float32)
    return value


def terms_kernel(bits, starts, prefactor, device, frequencies, *refs):
    sources = 4
    energies, refs = refs[:sources], refs[sources:]
    *groups, kept, sent, ordered, weighted = refs
    freqs = frequencies.shape[0]
    count = groups[0].shape[0]
    half = 1 << (bits - 1)
    rows = kept.shape[-2]
    me = device[0]
    across = me ^ jnp.where(me & 1, 2, 2 * half)
    owner = [me, me ^ 1, across, across ^ 1]
    held = [
        lambda spot: 2 * spot,
        lambda spot: 2 * reverse_bits(spot, bits) + 1,
        lambda spot: 2 * (spot ^ half),
        lambda spot: 2 * reverse_bits(spot ^ half, bits) + 1,
    ]
    total = [None, None]
    for q in range(sources):
        energy = energies[q][...]
        factors = []
        for w in range(freqs):
            square = frequencies[w] * frequencies[w]
            factors.append(-4.0 * energy / (energy * energy + square) * prefactor)
        for group, start in zip(groups[q::sources], starts):
            size = group.shape[1]
            for i in range(count):
                up, core = i >> 1, i & 1
                even, odd = 2 * up + core, 2 * reverse_bits(up, bits) + core
                piece = owner[q] ^ jnp.where(owner[q] & 1, odd, even)
                at = pl.multiple_of(piece * rows + start, 8)
                ordered[q % 2, pl.ds(at, size), :] = group[i].astype(jnp.float32)
            for spot in range(half):
                value = group[held[q](spot)].astype(jnp.float32)
                for w in range(freqs):
                    at = (spot * freqs + w) * rows + start
                    weighted[q % 2, at : at + size, :] = (value * factors[w]).astype(jnp.bfloat16)
        right = ordered[q % 2].astype(jnp.bfloat16)
        own = freqs * rows
        for k, part in enumerate((slice(own, half * own), slice(0, own))):
            if part.stop > part.start:
                term = lax.dot_general(
                    weighted[q % 2, part, :], right, NT, preferred_element_type=jnp.float32
                )
                total[k] = term if q == 0 else total[k] + term
    if half > 1:
        sent[...] = total[0].reshape(sent.shape)
    kept[...] = total[1].reshape(kept.shape)


def on_device(densities, eigen_basis, energies, frequencies):
    count = lax.axis_size("trans")
    bits = count.bit_length() - 2
    half = 1 << (bits - 1)
    states = densities.shape[0]
    rows = eigen_basis.shape[1]
    subspace = rows * count
    basis = eigen_basis.T
    spots = 1 << bits
    core_hop = [(d, d ^ 1) for d in range(count)]
    hops = [frame_hop(count, bits, bit) for bit in range(bits)]

    direct = [(across ^ 1, d) for d, across in hops[-1]]

    def from_sources(value):
        return [
            value,
            lax.ppermute(value, "trans", core_hop),
            lax.ppermute(value, "trans", hops[-1]),
            lax.ppermute(value, "trans", direct),
        ]

    energy = [value.reshape(1, states) for value in from_sources(energies)]
    prefactor = 1.0 / math.sqrt(states * count)

    operands, starts = [], []
    ranges = row_sections(rows)
    for number, (start, size, parts, blocks) in enumerate(ranges):
        waves = basis.shape[1] // parts
        sums = []
        for part in range(parts):
            mine = [basis[start : start + size, part * waves : part * waves + waves]]
            for spot in range(1, spots):
                low = (spot & -spot).bit_length() - 1
                mine.append(lax.ppermute(mine[spot & (spot - 1)], "trans", hops[low]))
            theirs = [lax.ppermute(mine[spot], "trans", core_hop) for spot in range(spots)]
            pieces = []
            for spot in range(spots):
                pieces += [mine[spot], theirs[reverse_bits(spot, bits)]]
            sums = project(pieces, densities, part * waves, blocks, sums)
        for block, value in enumerate(sums):
            projected = summed(value, "pw", number < len(ranges) - 1).astype(jnp.bfloat16)
            operands += from_sources(projected.reshape(count, size // blocks, states))
            starts.append(start + block * (size // blocks))
    freqs = frequencies.shape[0]
    kept, sent = pl.pallas_call(
        functools.partial(terms_kernel, bits, starts, prefactor),
        out_shape=(
            jax.ShapeDtypeStruct((freqs, rows, subspace), jnp.float32),
            jax.ShapeDtypeStruct((max(half - 1, 1), freqs, rows, subspace), jnp.float32),
        ),
        in_specs=[SMEM] * 2 + [VMEM] * (len(energy) + len(operands)),
        out_specs=(VMEM, VMEM),
        scratch_shapes=[
            pltpu.VMEM((2, subspace, states), jnp.float32),
            pltpu.VMEM((2, half * freqs * rows, states), jnp.bfloat16),
        ],
        compiler_params=pltpu.CompilerParams(vmem_limit_bytes=30 << 20),
    )(lax.axis_index("trans").astype(jnp.int32).reshape(1), frequencies, *energy, *operands)

    total = [kept] + [sent[i] for i in range(half - 1)]
    for bit in range(bits - 2, -1, -1):
        near = 1 << bit
        away = jnp.stack(total[near:]).astype(WIRE)
        got = lax.ppermute(away, "trans", hops[bit])
        total = [total[i] + got[i].astype(jnp.float32) for i in range(near)]
    return total[0]


def solution(mesh):
    placed = (P("trans", "pw"), P("pw", "trans"), P("trans"), P("pw"))
    return jax.shard_map(on_device, mesh=mesh, in_specs=placed, out_specs=P("pw", "trans", None), check_vma=False)
```

```python
import functools
import math

import jax
import jax.numpy as jnp
from jax import lax
from jax.experimental import pallas as pl
from jax.experimental.pallas import tpu as pltpu
from jax.sharding import PartitionSpec as P


NT = (((1,), (1,)), ((), ()))
VMEM = pl.BlockSpec(memory_space=pltpu.VMEM)
SMEM = pl.BlockSpec(memory_space=pltpu.SMEM)
HBM = pl.BlockSpec(memory_space=pltpu.HBM)
WIRE = jnp.bfloat16
SLOTS = 3


def reverse_bits(value, bits):
    return sum(((value >> i) & 1) << (bits - 1 - i) for i in range(bits))


def frame_hop(count, bits, bit):
    return [(d, d ^ (2 << (bits - 1 - bit if d & 1 else bit))) for d in range(count)]


def row_sections(rows):
    units = rows // 16
    if rows % 16 or units < 3:
        return [(0, rows, 1, 1)]
    sizes = [16 * (units // 3), 16 * max(1, units // 6)]
    first = rows - sum(sizes)
    return [(0, first, 1, 1), (first, sizes[0], 2, 1 if sizes[0] % 32 else 2), (first + sizes[0], sizes[1], 1, 1)]


def project_kernel(tile, first, blocks, resumed, *refs):
    *pieces, densities = refs[: -blocks - 3]
    outs, (held, arrived, total) = refs[-blocks - 3 : -3], refs[-3:]
    pieces, before = pieces[: len(pieces) - resumed], pieces[len(pieces) - resumed :]
    steps = pieces[0].shape[1] // tile
    size = pieces[0].shape[0] // blocks
    rows = size * len(pieces)

    def fetch(i, slot):
        at = pl.ds(pl.multiple_of(first + i * tile, tile), tile)
        return pltpu.make_async_copy(densities.at[:, at], held.at[slot], arrived.at[slot])

    for i in range(min(SLOTS - 1, steps)):
        fetch(i, i).start()
    for block in range(blocks):
        at = slice(block * rows, block * rows + rows)
        total[at, :] = before[block][...] if resumed else jnp.zeros((rows, total.shape[1]), total.dtype)

    def step(i, carry):
        slot = lax.rem(i, SLOTS)
        ahead = i + SLOTS - 1

        @pl.when(ahead < steps)
        def _():
            fetch(ahead, lax.rem(ahead, SLOTS)).start()

        fetch(i, slot).wait()
        at = pl.ds(pl.multiple_of(i * tile, tile), tile)
        basis = jnp.concatenate(
            [piece[b * size : b * size + size, at] for b in range(blocks) for piece in pieces], axis=0
        )
        total[...] += lax.dot_general(basis, held[slot], NT, preferred_element_type=jnp.float32)
        return carry

    lax.fori_loop(0, steps, step, 0)
    for block in range(blocks):
        outs[block][...] = total[block * rows : block * rows + rows, :]


def project(pieces, densities, first, blocks, before):
    rows = len(pieces) * pieces[0].shape[0]
    states, waves = densities.shape[0], pieces[0].shape[1]
    tile = math.gcd(waves, 2048)
    return pl.pallas_call(
        functools.partial(project_kernel, tile, first, blocks, len(before)),
        out_shape=[jax.ShapeDtypeStruct((rows // blocks, states), jnp.float32)] * blocks,
        in_specs=[VMEM] * (len(pieces) + len(before)) + [HBM],
        out_specs=[VMEM] * blocks,
        scratch_shapes=[
            pltpu.VMEM((SLOTS, states, tile), densities.dtype),
            pltpu.SemaphoreType.DMA((SLOTS,)),
            pltpu.VMEM((rows, states), jnp.float32),
        ],
        compiler_params=pltpu.CompilerParams(vmem_limit_bytes=(46 << 20) - min(rows * waves, 12 << 20)),
        cost_estimate=pl.CostEstimate(
            flops=2 * rows * states * waves,
            bytes_accessed=2 * waves * (rows + states),
            transcendentals=0,
        ),
    )(*pieces, *before, densities)


def summed(value, axis, far_first):
    count = lax.axis_size(axis)
    if count & (count - 1):
        return lax.psum(value, axis)
    bits = list(range(count.bit_length() - 1))
    for bit in bits[::-1] if far_first else bits:
        pairs = [(d, d ^ (1 << bit)) for d in range(count)]
        moved = lax.ppermute(value.astype(WIRE), axis, pairs)
        value = value + moved.astype(jnp.float32)
    return value


def lay_out(bits, rows, starts, prefactor, device, frequencies, energies, groups, ordered, weighted):
    sources, freqs = len(energies), frequencies.shape[0]
    count, half = 2 << bits, 1 << (bits - 1)
    aligned = 16 if ordered.dtype == jnp.bfloat16 else 8
    me = device[0]
    across = me ^ jnp.where(me & 1, 2, 2 * half)
    owner = [me, me ^ 1, across, across ^ 1]
    held = [
        lambda spot: 2 * spot,
        lambda spot: 2 * reverse_bits(spot, bits) + 1,
        lambda spot: 2 * (spot ^ half),
        lambda spot: 2 * reverse_bits(spot ^ half, bits) + 1,
    ]
    for q in range(sources):
        energy = energies[q][...]
        factors = []
        for w in range(freqs):
            square = frequencies[w] * frequencies[w]
            factors.append(-4.0 * energy / (energy * energy + square) * prefactor)
        for group, start in zip(groups[q::sources], starts):
            size = group.shape[1]
            for i in range(count):
                up, core = i >> 1, i & 1
                even, odd = 2 * up + core, 2 * reverse_bits(up, bits) + core
                piece = owner[q] ^ jnp.where(owner[q] & 1, odd, even)
                at = pl.multiple_of(piece * rows + start, aligned)
                ordered[q, pl.ds(at, size), :] = group[i].astype(ordered.dtype)
            for spot in range(half):
                value = group[held[q](spot)].astype(jnp.float32)
                for w in range(freqs):
                    at = (spot * freqs + w) * rows + start
                    weighted[q, at : at + size, :] = (value * factors[w]).astype(jnp.bfloat16)


def early_kernel(bits, rows, starts, prefactor, device, frequencies, *refs):
    energies, groups, (ordered, weighted) = refs[:4], refs[4:-2], refs[-2:]
    lay_out(bits, rows, starts, prefactor, device, frequencies, energies, groups, ordered, weighted)


def terms_kernel(bits, rows, starts, prefactor, device, frequencies, *refs):
    energies, groups = refs[:4], refs[4 : 4 + 4 * len(starts)]
    kept, sent, ordered, weighted = refs[-4:]
    lay_out(bits, rows, starts, prefactor, device, frequencies, energies, groups, ordered, weighted)
    total = None
    for q in range(len(energies)):
        right = ordered[q].astype(jnp.bfloat16)
        term = lax.dot_general(weighted[q], right, NT, preferred_element_type=jnp.float32)
        total = term if q == 0 else total + term
    own = kept.shape[0] * rows
    if total.shape[0] > own:
        sent[...] = total[own:].reshape(sent.shape)
    kept[...] = total[:own].reshape(kept.shape)


def on_device(densities, eigen_basis, energies, frequencies):
    count = lax.axis_size("trans")
    bits = count.bit_length() - 2
    half = 1 << (bits - 1)
    states = densities.shape[0]
    rows = eigen_basis.shape[1]
    subspace = rows * count
    basis = eigen_basis.T
    spots = 1 << bits
    core_hop = [(d, d ^ 1) for d in range(count)]
    hops = [frame_hop(count, bits, bit) for bit in range(bits)]

    direct = [(across ^ 1, d) for d, across in hops[-1]]

    def from_sources(value):
        return [
            value,
            lax.ppermute(value, "trans", core_hop),
            lax.ppermute(value, "trans", hops[-1]),
            lax.ppermute(value, "trans", direct),
        ]

    energy = [value.reshape(1, states) for value in from_sources(energies)]
    prefactor = 1.0 / math.sqrt(states * count)

    operands, starts = [], []
    ranges = row_sections(rows)
    for number, (start, size, parts, blocks) in enumerate(ranges):
        waves = basis.shape[1] // parts
        sums = []
        for part in range(parts):
            mine = [basis[start : start + size, part * waves : part * waves + waves]]
            for spot in range(1, spots):
                low = (spot & -spot).bit_length() - 1
                mine.append(lax.ppermute(mine[spot & (spot - 1)], "trans", hops[low]))
            theirs = [lax.ppermute(mine[spot], "trans", core_hop) for spot in range(spots)]
            pieces = []
            for spot in range(spots):
                pieces += [mine[spot], theirs[reverse_bits(spot, bits)]]
            sums = project(pieces, densities, part * waves, blocks, sums)
        for block, value in enumerate(sums):
            projected = summed(value, "pw", number < len(ranges) - 1).astype(jnp.bfloat16)
            operands += from_sources(projected.reshape(count, size // blocks, states))
            starts.append(start + block * (size // blocks))
    freqs = frequencies.shape[0]
    fits = rows % 16 == 0 and not any(start % 16 for start in starts)
    buffers = (
        jax.ShapeDtypeStruct((4, subspace, states), jnp.bfloat16 if fits else jnp.float32),
        jax.ShapeDtypeStruct((4, half * freqs * rows, states), jnp.bfloat16),
    )
    common = [lax.axis_index("trans").astype(jnp.int32).reshape(1), frequencies, *energy]
    specs = [SMEM] * 2 + [VMEM] * len(energy)
    split = max(len(starts) - 2, 0)
    early = []
    if split:
        early = pl.pallas_call(
            functools.partial(early_kernel, bits, rows, starts[:split], prefactor),
            out_shape=buffers,
            in_specs=specs + [VMEM] * (4 * split),
            out_specs=(VMEM, VMEM),
            compiler_params=pltpu.CompilerParams(vmem_limit_bytes=16 << 20),
        )(*common, *operands[: 4 * split])
    late = [*common, *operands[4 * split :], *early]
    kept, sent, _, _ = pl.pallas_call(
        functools.partial(terms_kernel, bits, rows, starts[split:], prefactor),
        out_shape=(
            jax.ShapeDtypeStruct((freqs, rows, subspace), jnp.float32),
            jax.ShapeDtypeStruct((max(half - 1, 1), freqs, rows, subspace), jnp.float32),
            *buffers,
        ),
        in_specs=specs + [VMEM] * (len(late) - len(common)),
        out_specs=(VMEM,) * 4,
        input_output_aliases={len(late) - 2: 2, len(late) - 1: 3} if split else {},
        compiler_params=pltpu.CompilerParams(vmem_limit_bytes=24 << 20),
    )(*late)

    total = [kept] + [sent[i] for i in range(half - 1)]
    for bit in range(bits - 2, -1, -1):
        near = 1 << bit
        away = jnp.stack(total[near:]).astype(WIRE)
        got = lax.ppermute(away, "trans", hops[bit])
        total = [total[i] + got[i].astype(jnp.float32) for i in range(near)]
    return total[0]


def solution(mesh):
    placed = (P("trans", "pw"), P("pw", "trans"), P("trans"), P("pw"))
    return jax.shard_map(on_device, mesh=mesh, in_specs=placed, out_specs=P("pw", "trans", None), check_vma=False)
```

```python
import functools
import math

import jax
import jax.numpy as jnp
from jax import lax
from jax.experimental import pallas as pl
from jax.experimental.pallas import tpu as pltpu
from jax.sharding import PartitionSpec as P


NT = (((1,), (1,)), ((), ()))
VMEM = pl.BlockSpec(memory_space=pltpu.VMEM)
SMEM = pl.BlockSpec(memory_space=pltpu.SMEM)
HBM = pl.BlockSpec(memory_space=pltpu.HBM)
WIRE = jnp.bfloat16
SLOTS = 3


def reverse_bits(value, bits):
    return sum(((value >> i) & 1) << (bits - 1 - i) for i in range(bits))


def frame_hop(count, bits, bit):
    return [(d, d ^ (2 << (bits - 1 - bit if d & 1 else bit))) for d in range(count)]


def row_sections(rows):
    units = rows // 16
    if rows % 16 or units < 3:
        return [(0, rows, 1, 1)]
    sizes = [16 * (units // 3), 16 * max(1, units // 6)]
    first = rows - sum(sizes)
    return [(0, first, 1, 1), (first, sizes[0], 2, 1 if sizes[0] % 32 else 2), (first + sizes[0], sizes[1], 1, 1)]


def project_kernel(tile, first, blocks, resumed, turned, *refs):
    *pieces, densities = refs[: -blocks - 3]
    outs, (held, arrived, total) = refs[-blocks - 3 : -3], refs[-3:]
    pieces, before = pieces[: len(pieces) - resumed], pieces[len(pieces) - resumed :]
    steps = pieces[0].shape[1] // tile
    size = pieces[0].shape[0] // blocks
    rows = size * len(pieces)

    def fetch(i, slot):
        at = pl.ds(pl.multiple_of(first + i * tile, tile), tile)
        return pltpu.make_async_copy(densities.at[:, at], held.at[slot], arrived.at[slot])

    for i in range(min(SLOTS - 1, steps)):
        fetch(i, i).start()
    if not resumed:
        total[...] = jnp.zeros_like(total)
    for block in range(resumed):
        total[block * rows : block * rows + rows, :] = before[block][...]

    def step(i, carry):
        slot = lax.rem(i, SLOTS)
        ahead = i + SLOTS - 1

        @pl.when(ahead < steps)
        def _():
            fetch(ahead, lax.rem(ahead, SLOTS)).start()

        fetch(i, slot).wait()
        at = pl.ds(pl.multiple_of(i * tile, tile), tile)
        basis = jnp.concatenate(
            [piece[b * size : b * size + size, at] for b in range(blocks) for piece in pieces], axis=0
        )
        sides = (held[slot], basis) if turned else (basis, held[slot])
        total[...] += lax.dot_general(*sides, NT, preferred_element_type=jnp.float32)
        return carry

    lax.fori_loop(0, steps, step, 0)
    if turned:
        outs[0][...] = total[...].T
        return
    for block in range(blocks):
        outs[block][...] = total[block * rows : block * rows + rows, :]


def project(pieces, densities, first, blocks, before):
    rows = len(pieces) * pieces[0].shape[0]
    states, waves = densities.shape[0], pieces[0].shape[1]
    turned = rows <= 128 and blocks == 1 and not before
    tile = math.gcd(waves, 4096 if turned else 2048)
    return pl.pallas_call(
        functools.partial(project_kernel, tile, first, blocks, len(before), turned),
        out_shape=[jax.ShapeDtypeStruct((rows // blocks, states), jnp.float32)] * blocks,
        in_specs=[VMEM] * (len(pieces) + len(before)) + [HBM],
        out_specs=[VMEM] * blocks,
        scratch_shapes=[
            pltpu.VMEM((SLOTS, states, tile), densities.dtype),
            pltpu.SemaphoreType.DMA((SLOTS,)),
            pltpu.VMEM((states, rows) if turned else (rows, states), jnp.float32),
        ],
        compiler_params=pltpu.CompilerParams(vmem_limit_bytes=(46 << 20) - min(rows * waves, 12 << 20)),
        cost_estimate=pl.CostEstimate(
            flops=2 * rows * states * waves,
            bytes_accessed=2 * waves * (rows + states),
            transcendentals=0,
        ),
    )(*pieces, *before, densities)


def summed(value, axis, far_first):
    count = lax.axis_size(axis)
    if count & (count - 1):
        return lax.psum(value, axis)
    bits = list(range(count.bit_length() - 1))
    for bit in bits[::-1] if far_first else bits:
        pairs = [(d, d ^ (1 << bit)) for d in range(count)]
        moved = lax.ppermute(value.astype(WIRE), axis, pairs)
        value = value + moved.astype(jnp.float32)
    return value


def lay_out(bits, rows, starts, prefactor, device, frequencies, energies, groups, ordered, weighted):
    sources, freqs = len(energies), frequencies.shape[0]
    count, half = 2 << bits, 1 << (bits - 1)
    aligned = 16 if ordered.dtype == jnp.bfloat16 else 8
    me = device[0]
    across = me ^ jnp.where(me & 1, 2, 2 * half)
    owner = [me, me ^ 1, across, across ^ 1]
    held = [
        lambda spot: 2 * spot,
        lambda spot: 2 * reverse_bits(spot, bits) + 1,
        lambda spot: 2 * (spot ^ half),
        lambda spot: 2 * reverse_bits(spot ^ half, bits) + 1,
    ]
    for q in range(sources):
        energy = energies[q][...]
        factors = []
        for w in range(freqs):
            square = frequencies[w] * frequencies[w]
            factors.append(-4.0 * energy / (energy * energy + square) * prefactor)
        for group, start in zip(groups[q::sources], starts):
            size = group.shape[1]
            for i in range(count):
                up, core = i >> 1, i & 1
                even, odd = 2 * up + core, 2 * reverse_bits(up, bits) + core
                piece = owner[q] ^ jnp.where(owner[q] & 1, odd, even)
                at = pl.multiple_of(piece * rows + start, aligned)
                ordered[q, pl.ds(at, size), :] = group[i].astype(ordered.dtype)
            for spot in range(half):
                value = group[held[q](spot)].astype(jnp.float32)
                for w in range(freqs):
                    at = (spot * freqs + w) * rows + start
                    weighted[q, at : at + size, :] = (value * factors[w]).astype(jnp.bfloat16)


def early_kernel(bits, rows, starts, prefactor, device, frequencies, *refs):
    energies, groups, (ordered, weighted) = refs[:4], refs[4:-2], refs[-2:]
    lay_out(bits, rows, starts, prefactor, device, frequencies, energies, groups, ordered, weighted)


def terms_kernel(bits, rows, starts, prefactor, device, frequencies, *refs):
    energies, groups = refs[:4], refs[4 : 4 + 4 * len(starts)]
    kept, sent, ordered, weighted = refs[-4:]
    lay_out(bits, rows, starts, prefactor, device, frequencies, energies, groups, ordered, weighted)
    total = None
    for q in range(len(energies)):
        right = ordered[q].astype(jnp.bfloat16)
        term = lax.dot_general(weighted[q], right, NT, preferred_element_type=jnp.float32)
        total = term if q == 0 else total + term
    own = kept.shape[0] * rows
    if total.shape[0] > own:
        sent[...] = total[own:].reshape(sent.shape)
    kept[...] = total[:own].reshape(kept.shape)


def on_device(densities, eigen_basis, energies, frequencies):
    count = lax.axis_size("trans")
    bits = count.bit_length() - 2
    half = 1 << (bits - 1)
    states = densities.shape[0]
    rows = eigen_basis.shape[1]
    subspace = rows * count
    basis = eigen_basis.T
    spots = 1 << bits
    core_hop = [(d, d ^ 1) for d in range(count)]
    hops = [frame_hop(count, bits, bit) for bit in range(bits)]

    direct = [(across ^ 1, d) for d, across in hops[-1]]

    def from_sources(value):
        return [
            value,
            lax.ppermute(value, "trans", core_hop),
            lax.ppermute(value, "trans", hops[-1]),
            lax.ppermute(value, "trans", direct),
        ]

    energy = [value.reshape(1, states) for value in from_sources(energies)]
    prefactor = 1.0 / math.sqrt(states * count)

    operands, starts = [], []
    ranges = row_sections(rows)
    for number, (start, size, parts, blocks) in enumerate(ranges):
        waves = basis.shape[1] // parts
        sums = []
        for part in range(parts):
            mine = [basis[start : start + size, part * waves : part * waves + waves]]
            for spot in range(1, spots):
                low = (spot & -spot).bit_length() - 1
                mine.append(lax.ppermute(mine[spot & (spot - 1)], "trans", hops[low]))
            theirs = [lax.ppermute(mine[spot], "trans", core_hop) for spot in range(spots)]
            pieces = []
            for spot in range(spots):
                pieces += [mine[spot], theirs[reverse_bits(spot, bits)]]
            sums = project(pieces, densities, part * waves, blocks, sums)
        for block, value in enumerate(sums):
            projected = summed(value, "pw", number < len(ranges) - 1).astype(jnp.bfloat16)
            operands += from_sources(projected.reshape(count, size // blocks, states))
            starts.append(start + block * (size // blocks))
    freqs = frequencies.shape[0]
    fits = rows % 16 == 0 and not any(start % 16 for start in starts)
    buffers = (
        jax.ShapeDtypeStruct((4, subspace, states), jnp.bfloat16 if fits else jnp.float32),
        jax.ShapeDtypeStruct((4, half * freqs * rows, states), jnp.bfloat16),
    )
    common = [lax.axis_index("trans").astype(jnp.int32).reshape(1), frequencies, *energy]
    specs = [SMEM] * 2 + [VMEM] * len(energy)
    split = max(len(starts) - 2, 0)
    early = []
    if split:
        early = pl.pallas_call(
            functools.partial(early_kernel, bits, rows, starts[:split], prefactor),
            out_shape=buffers,
            in_specs=specs + [VMEM] * (4 * split),
            out_specs=(VMEM, VMEM),
            compiler_params=pltpu.CompilerParams(vmem_limit_bytes=16 << 20),
        )(*common, *operands[: 4 * split])
    late = [*common, *operands[4 * split :], *early]
    kept, sent, _, _ = pl.pallas_call(
        functools.partial(terms_kernel, bits, rows, starts[split:], prefactor),
        out_shape=(
            jax.ShapeDtypeStruct((freqs, rows, subspace), jnp.float32),
            jax.ShapeDtypeStruct((max(half - 1, 1), freqs, rows, subspace), jnp.float32),
            *buffers,
        ),
        in_specs=specs + [VMEM] * (len(late) - len(common)),
        out_specs=(VMEM,) * 4,
        input_output_aliases={len(late) - 2: 2, len(late) - 1: 3} if split else {},
        compiler_params=pltpu.CompilerParams(vmem_limit_bytes=24 << 20),
    )(*late)

    total = [kept] + [sent[i] for i in range(half - 1)]
    for bit in range(bits - 2, -1, -1):
        near = 1 << bit
        away = jnp.stack(total[near:]).astype(WIRE)
        got = lax.ppermute(away, "trans", hops[bit])
        total = [total[i] + got[i].astype(jnp.float32) for i in range(near)]
    return total[0]


def solution(mesh):
    placed = (P("trans", "pw"), P("pw", "trans"), P("trans"), P("pw"))
    return jax.shard_map(on_device, mesh=mesh, in_specs=placed, out_specs=P("pw", "trans", None), check_vma=False)
```

```python
import functools
import math

import jax
import jax.numpy as jnp
from jax import lax
from jax.experimental import pallas as pl
from jax.experimental.pallas import tpu as pltpu
from jax.sharding import PartitionSpec as P


NT = (((1,), (1,)), ((), ()))
VMEM = pl.BlockSpec(memory_space=pltpu.VMEM)
SMEM = pl.BlockSpec(memory_space=pltpu.SMEM)
HBM = pl.BlockSpec(memory_space=pltpu.HBM)
WIRE = jnp.bfloat16
SLOTS = 3


def reverse_bits(value, bits):
    return sum(((value >> i) & 1) << (bits - 1 - i) for i in range(bits))


def frame_hop(count, bits, bit):
    return [(d, d ^ (2 << (bits - 1 - bit if d & 1 else bit))) for d in range(count)]


def row_sections(rows):
    units = rows // 16
    if rows % 16 or units < 3:
        return [(0, rows, 1, 1)]
    sizes = [16 * (units // 3), 16 * max(1, units // 6)]
    first = rows - sum(sizes)
    return [(0, first, 2, 1), (first, sizes[0], 2, 1 if sizes[0] % 32 else 2), (first + sizes[0], sizes[1], 1, 1)]


def project_kernel(tile, first, blocks, resumed, turned, *refs):
    *pieces, densities = refs[: -blocks - 3]
    outs, (held, arrived, total) = refs[-blocks - 3 : -3], refs[-3:]
    pieces, before = pieces[: len(pieces) - resumed], pieces[len(pieces) - resumed :]
    steps = pieces[0].shape[1] // tile
    size = pieces[0].shape[0] // blocks
    rows = size * len(pieces)

    def fetch(i, slot):
        at = pl.ds(pl.multiple_of(first + i * tile, tile), tile)
        return pltpu.make_async_copy(densities.at[:, at], held.at[slot], arrived.at[slot])

    for i in range(min(SLOTS - 1, steps)):
        fetch(i, i).start()
    if not resumed:
        total[...] = jnp.zeros_like(total)
    for block in range(resumed):
        total[block * rows : block * rows + rows, :] = before[block][...]

    def step(i, carry):
        slot = lax.rem(i, SLOTS)
        ahead = i + SLOTS - 1

        @pl.when(ahead < steps)
        def _():
            fetch(ahead, lax.rem(ahead, SLOTS)).start()

        fetch(i, slot).wait()
        at = pl.ds(pl.multiple_of(i * tile, tile), tile)
        basis = jnp.concatenate(
            [piece[b * size : b * size + size, at] for b in range(blocks) for piece in pieces], axis=0
        )
        sides = (held[slot], basis) if turned else (basis, held[slot])
        total[...] += lax.dot_general(*sides, NT, preferred_element_type=jnp.float32)
        return carry

    lax.fori_loop(0, steps, step, 0)
    if turned:
        outs[0][...] = total[...].T
        return
    for block in range(blocks):
        outs[block][...] = total[block * rows : block * rows + rows, :]


def project(pieces, densities, first, blocks, before, grant):
    rows = len(pieces) * pieces[0].shape[0]
    states, waves = densities.shape[0], pieces[0].shape[1]
    turned = rows <= 128 and blocks == 1 and not before
    tile = math.gcd(waves, 4096 if turned else 2048)
    return pl.pallas_call(
        functools.partial(project_kernel, tile, first, blocks, len(before), turned),
        out_shape=[jax.ShapeDtypeStruct((rows // blocks, states), jnp.float32)] * blocks,
        in_specs=[VMEM] * (len(pieces) + len(before)) + [HBM],
        out_specs=[VMEM] * blocks,
        scratch_shapes=[
            pltpu.VMEM((SLOTS, states, tile), densities.dtype),
            pltpu.SemaphoreType.DMA((SLOTS,)),
            pltpu.VMEM((states, rows) if turned else (rows, states), jnp.float32),
        ],
        compiler_params=pltpu.CompilerParams(vmem_limit_bytes=grant),
        cost_estimate=pl.CostEstimate(
            flops=2 * rows * states * waves,
            bytes_accessed=2 * waves * (rows + states),
            transcendentals=0,
        ),
    )(*pieces, *before, densities)


def summed(value, axis, far_first):
    count = lax.axis_size(axis)
    if count & (count - 1):
        return lax.psum(value, axis)
    bits = list(range(count.bit_length() - 1))
    for bit in bits[::-1] if far_first else bits:
        pairs = [(d, d ^ (1 << bit)) for d in range(count)]
        moved = lax.ppermute(value.astype(WIRE), axis, pairs)
        value = value + moved.astype(jnp.float32)
    return value


def lay_out(bits, rows, starts, prefactor, device, frequencies, energies, groups, ordered, weighted):
    sources, freqs = len(energies), frequencies.shape[0]
    count, half = 2 << bits, 1 << (bits - 1)
    aligned = 16 if ordered.dtype == jnp.bfloat16 else 8
    me = device[0]
    across = me ^ jnp.where(me & 1, 2, 2 * half)
    owner = [me, me ^ 1, across, across ^ 1]
    held = [
        lambda spot: 2 * spot,
        lambda spot: 2 * reverse_bits(spot, bits) + 1,
        lambda spot: 2 * (spot ^ half),
        lambda spot: 2 * reverse_bits(spot ^ half, bits) + 1,
    ]
    for q in range(sources):
        energy = energies[q][...]
        factors = []
        for w in range(freqs):
            square = frequencies[w] * frequencies[w]
            factors.append(-4.0 * energy / (energy * energy + square) * prefactor)
        for group, start in zip(groups[q::sources], starts):
            size = group.shape[1]
            for i in range(count):
                up, core = i >> 1, i & 1
                even, odd = 2 * up + core, 2 * reverse_bits(up, bits) + core
                piece = owner[q] ^ jnp.where(owner[q] & 1, odd, even)
                at = pl.multiple_of(piece * rows + start, aligned)
                ordered[q, pl.ds(at, size), :] = group[i].astype(ordered.dtype)
            for spot in range(half):
                value = group[held[q](spot)].astype(jnp.float32)
                for w in range(freqs):
                    at = (spot * freqs + w) * rows + start
                    weighted[q, at : at + size, :] = (value * factors[w]).astype(jnp.bfloat16)


def early_kernel(bits, rows, starts, prefactor, device, frequencies, *refs):
    energies, groups, (ordered, weighted) = refs[:4], refs[4:-2], refs[-2:]
    lay_out(bits, rows, starts, prefactor, device, frequencies, energies, groups, ordered, weighted)


def terms_kernel(bits, rows, starts, prefactor, device, frequencies, *refs):
    energies, groups = refs[:4], refs[4 : 4 + 4 * len(starts)]
    kept, sent, ordered, weighted = refs[-4:]
    lay_out(bits, rows, starts, prefactor, device, frequencies, energies, groups, ordered, weighted)
    total = None
    for q in range(len(energies)):
        right = ordered[q].astype(jnp.bfloat16)
        term = lax.dot_general(weighted[q], right, NT, preferred_element_type=jnp.float32)
        total = term if q == 0 else total + term
    own = kept.shape[0] * rows
    if total.shape[0] > own:
        sent[...] = total[own:].reshape(sent.shape)
    kept[...] = total[:own].reshape(kept.shape)


def on_device(densities, eigen_basis, energies, frequencies):
    count = lax.axis_size("trans")
    bits = count.bit_length() - 2
    half = 1 << (bits - 1)
    states = densities.shape[0]
    rows = eigen_basis.shape[1]
    subspace = rows * count
    basis = eigen_basis.T
    spots = 1 << bits
    core_hop = [(d, d ^ 1) for d in range(count)]
    hops = [frame_hop(count, bits, bit) for bit in range(bits)]

    direct = [(across ^ 1, d) for d, across in hops[-1]]

    def from_sources(value):
        return [
            value,
            lax.ppermute(value, "trans", core_hop),
            lax.ppermute(value, "trans", hops[-1]),
            lax.ppermute(value, "trans", direct),
        ]

    energy = [value.reshape(1, states) for value in from_sources(energies)]
    prefactor = 1.0 / math.sqrt(states * count)

    operands, starts = [], []
    ranges = row_sections(rows)
    for number, (start, size, parts, blocks) in enumerate(ranges):
        waves = basis.shape[1] // parts
        sums = []
        for part in range(parts):
            mine = [basis[start : start + size, part * waves : part * waves + waves]]
            if number == part == 0:
                basis, mine[0] = lax.optimization_barrier((basis, mine[0]))
            for spot in range(1, spots):
                low = (spot & -spot).bit_length() - 1
                mine.append(lax.ppermute(mine[spot & (spot - 1)], "trans", hops[low]))
            theirs = [lax.ppermute(mine[spot], "trans", core_hop) for spot in range(spots)]
            pieces = []
            for spot in range(spots):
                pieces += [mine[spot], theirs[reverse_bits(spot, bits)]]
            sums = project(pieces, densities, part * waves, blocks, sums, (44 if number else 34) << 20)
        for block, value in enumerate(sums):
            projected = summed(value, "pw", number < len(ranges) - 1).astype(jnp.bfloat16)
            operands += from_sources(projected.reshape(count, size // blocks, states))
            starts.append(start + block * (size // blocks))
    freqs = frequencies.shape[0]
    fits = rows % 16 == 0 and not any(start % 16 for start in starts)
    buffers = (
        jax.ShapeDtypeStruct((4, subspace, states), jnp.bfloat16 if fits else jnp.float32),
        jax.ShapeDtypeStruct((4, half * freqs * rows, states), jnp.bfloat16),
    )
    common = [lax.axis_index("trans").astype(jnp.int32).reshape(1), frequencies, *energy]
    specs = [SMEM] * 2 + [VMEM] * len(energy)
    split = max(len(starts) - 2, 0)
    early = []
    if split:
        early = pl.pallas_call(
            functools.partial(early_kernel, bits, rows, starts[:split], prefactor),
            out_shape=buffers,
            in_specs=specs + [VMEM] * (4 * split),
            out_specs=(VMEM, VMEM),
            compiler_params=pltpu.CompilerParams(vmem_limit_bytes=16 << 20),
        )(*common, *operands[: 4 * split])
    late = [*common, *operands[4 * split :], *early]
    kept, sent, _, _ = pl.pallas_call(
        functools.partial(terms_kernel, bits, rows, starts[split:], prefactor),
        out_shape=(
            jax.ShapeDtypeStruct((freqs, rows, subspace), jnp.float32),
            jax.ShapeDtypeStruct((max(half - 1, 1), freqs, rows, subspace), jnp.float32),
            *buffers,
        ),
        in_specs=specs + [VMEM] * (len(late) - len(common)),
        out_specs=(VMEM,) * 4,
        input_output_aliases={len(late) - 2: 2, len(late) - 1: 3} if split else {},
        compiler_params=pltpu.CompilerParams(vmem_limit_bytes=24 << 20),
    )(*late)

    total = [kept] + [sent[i] for i in range(half - 1)]
    for bit in range(bits - 2, -1, -1):
        near = 1 << bit
        away = jnp.stack(total[near:]).astype(WIRE)
        got = lax.ppermute(away, "trans", hops[bit])
        total = [total[i] + got[i].astype(jnp.float32) for i in range(near)]
    return total[0]


def solution(mesh):
    placed = (P("trans", "pw"), P("pw", "trans"), P("trans"), P("pw"))
    return jax.shard_map(on_device, mesh=mesh, in_specs=placed, out_specs=P("pw", "trans", None), check_vma=False)
```
